256 devices in a mesh: lon: 32 (over z, x_lo, core), obs: 8 (over x_hi, y).
Axes of the slice: x: 4 (x_hi: 2, x_lo: 2; x = x_hi * 2 + x_lo), y: 4, z: 8, core: 2. Of those that a mesh axis runs over, the one named last changes fastest.
Arguments:
- perturb: float32 [32768, 1024], P('lon'), may hold values from -6 to 6
- observed: bfloat16 [32768, 1024], P(('lon', 'obs')), may hold values from -6 to 6
- solved: bfloat16 [32768, 1024], P(('lon', 'obs')), may hold values from -6 to 6
- taper_index: int32 [32768, 7168], P('lon', 'obs'), may hold values from 0 to 15
- taper_table: float32 [16], replicated, may hold values from 0.05 to 1
Outputs:
- analysis: float32 [32768, 1024], P(('lon', 'obs'))
The draws below stay inside these ranges and needn't reach their ends.
All inputs are finite; a program needn't handle non-finite values.
Results may differ from the reference program's by a relative error of at most 0.0035.
Values may be sent and summed in bfloat16 or wider, within the bound.
A program may use at most 128 MiB of HBM per device.

```python
import math
import jax
import jax.numpy as jnp
from jax import lax

MEMBERS = 1024
PTS_TILE = 1024
OBS_DEV = 128
REACH = 3
LEVELS = 16
NPTS = 32768
NOBS = 32768
WINDOW = 7168
N_LON = 32
N_OBS = 8


def touch_ends(entries, stream_key, low, high):
    longest = entries.shape.index(max(entries.shape))
    spots = []
    for shift in (0, 1):
        where = [jax.random.randint(jax.random.fold_in(stream_key, axis), (), 0, length) for axis, length in enumerate(entries.shape)]
        where[longest] = (where[longest] + shift) % entries.shape[longest]
        spots.append(tuple(where))
    return entries.at[spots[0]].set(low).at[spots[1]].set(high)


def levels(stream_key, extent, cuts, least, largest):
    gain, own = 1.0, jax.random.fold_in(stream_key, 6)
    for axis_at, shards_of in cuts:
        draws = jnp.exp(jax.random.uniform(jax.random.fold_in(own, axis_at), (shards_of,), jnp.float32, least / len(cuts), largest / len(cuts)))
        gain = gain * jnp.repeat(draws, extent[axis_at] // shards_of).reshape([-1 if axis == axis_at else 1 for axis in range(len(extent))])
    return gain


def centred(rng, dims, spread, most, cuts=(), kind=jnp.bfloat16):
    array = spread * jax.random.normal(rng, dims, jnp.float32)
    if cuts:
        array = array * levels(rng, dims, cuts, -0.22, 0.18)
    return jnp.clip(array, -most, most).astype(kind)


def setup_inputs(seed: int = 0) -> dict:
    arg_keys = jax.random.split(jax.random.key(seed), 6)
    perturb = centred(arg_keys[0], (NPTS, MEMBERS), 1.0, 6.0, ((0, 32),), jnp.float32)
    observed = centred(arg_keys[1], (NOBS, MEMBERS), 1.0, 6.0, ((0, 256),))
    solved = centred(arg_keys[2], (NOBS, MEMBERS), 1.0, 6.0, ((0, 256),))
    taper_index = touch_ends(jax.random.randint(arg_keys[3], (NPTS, WINDOW), 0, LEVELS), jax.random.fold_in(arg_keys[3], 1), 0, LEVELS - 1).astype(jnp.int32)
    taper_table = jnp.clip(jnp.exp(jax.random.uniform(arg_keys[4], (LEVELS,), jnp.float32, math.log(0.05), math.log(1.0))), 0.05, 1.0)
    return dict(perturb=perturb, observed=observed, solved=solved, taper_index=taper_index, taper_table=taper_table)


def reference(perturb, observed, solved, taper_index, taper_table):
    span = 2 * REACH + 1
    obs_four = observed.reshape(N_LON, N_OBS, OBS_DEV, MEMBERS)
    sol_four = solved.reshape(N_LON, N_OBS, OBS_DEV, MEMBERS)
    tiles_x = perturb.reshape(N_LON, PTS_TILE, MEMBERS)
    tiles_i = taper_index.reshape(N_LON, PTS_TILE, N_OBS * span * OBS_DEV)

    def one_tile(packed):
        tile, xs, index_tile = packed
        near = (tile + jnp.arange(span, dtype=jnp.int32) - REACH) % N_LON
        y_win = jnp.transpose(obs_four[near], (1, 0, 2, 3)).reshape(-1, MEMBERS).astype(jnp.float32)
        z_win = jnp.transpose(sol_four[near], (1, 0, 2, 3)).reshape(-1, MEMBERS).astype(jnp.float32)
        x_half = xs.astype(jnp.bfloat16)
        x_half = lax.optimization_barrier(x_half).astype(jnp.float32)
        cov = jnp.dot(x_half, y_win.T, precision=lax.Precision.HIGHEST) / (MEMBERS - 1)
        rho = taper_table[index_tile]
        weighted = (rho * cov).astype(jnp.bfloat16)
        weighted = lax.optimization_barrier(weighted).astype(jnp.float32)
        return xs + jnp.dot(weighted, z_win, precision=lax.Precision.HIGHEST)

    result = lax.map(one_tile, (jnp.arange(N_LON, dtype=jnp.int32), tiles_x, tiles_i))
    return result.reshape(N_LON * PTS_TILE, MEMBERS)
```

```python
import functools

import jax
import jax.numpy as jnp
from jax import lax
from jax.experimental import pallas as pl
from jax.experimental.pallas import tpu as pltpu
from jax.sharding import Mesh
from jax.sharding import PartitionSpec as P

MESH = pl.DeviceIdType.MESH
BF16, F32 = jnp.bfloat16, jnp.float32
SLOTS = 7
CUTS = 2
PARTS = 4
OUTER = (0, 1, 2, 3, -3, -2, -1)
INNER = (0, -1, 2, 1, 3, -2, -3)


def kernel(
    perturb, observed, solved, taper_index, table, out,
    x_full, x_half, obs, sol, index, rho, weighted, part, passed, joined, came, half_out, half_in, half_own, result,
    load_sem, obs_load_sem, sol_load_sem, index_sem, out_sem,
    obs_send, obs_recv, sol_send, sol_recv, y_send, y_recv, x_send, x_recv,
):
    z, xl, core, xh, y = (lax.axis_index(a) for a in ("z", "xl", "core", "xh", "y"))
    depth, ring = lax.axis_size("z"), lax.axis_size("y")
    rows, members = perturb.shape
    width = observed.shape[0]
    cut = width // CUTS
    span = members // PARTS
    share = rows // (2 * ring)
    way = 1 - 2 * xl
    side = 2 * core - 1
    inner = xl + core - 2 * xl * core

    mate = {"core": 1 - core}
    across = {"xl": 1 - xl}
    slant = {"z": lax.rem(z + side + depth, depth), "core": 1 - core}
    ahead = {"z": lax.rem(z + way + depth, depth)}
    behind = {"z": lax.rem(z - way + depth, depth)}
    y_up, y_down = lax.rem(y + 1, ring), lax.rem(y + ring - 1, ring)
    far = lax.rem(y + 2, ring)
    y_next = (y_up, y_down)
    opposite = {"xh": 1 - xh}

    step = rows // 4
    loads = [
        pltpu.make_async_copy(perturb.at[pl.ds(i * step, step)], x_full.at[pl.ds(i * step, step)], load_sem.at[i])
        for i in range(4)
    ]
    own_obs = pltpu.make_async_copy(observed, obs.at[0], obs_load_sem)
    own_sol = [
        pltpu.make_async_copy(solved.at[:, pl.ds(c * span, span)], sol.at[c, pl.ds(0, width)], sol_load_sem.at[c])
        for c in range(PARTS)
    ]
    index_loads = []
    for slot in range(SLOTS):
        offset = way * (OUTER[slot] + inner * (INNER[slot] - OUTER[slot]))
        start = pl.multiple_of((offset + SLOTS // 2) * width, width)
        index_loads.append(
            pltpu.make_async_copy(taper_index.at[:, pl.ds(start, width)], index.at[slot], index_sem.at[slot])
        )

    barrier = pltpu.get_barrier_semaphore()
    peers = (mate, across, slant, ahead, behind, {"y": y_up}, {"y": y_down}, opposite)
    for peer in peers:
        pl.semaphore_signal(barrier, inc=1, device_id=peer, device_id_type=MESH)
    own_obs.start()
    for i in range(4):
        loads[i].start()
    for slot in (0, 1, 4, 2, 3, 5, 6):
        index_loads[slot].start()
    for c in range(PARTS):
        own_sol[c].start()
    pl.semaphore_wait(barrier, len(peers))

    def remote(src, dst, send, recv, peer):
        return pltpu.make_async_remote_copy(
            src_ref=src, dst_ref=dst, send_sem=send, recv_sem=recv, device_id=peer, device_id_type=MESH
        )

    routes = {1: (0, mate), 2: (0, across), 3: (2, mate), 4: (0, slant), 5: (2, ahead), 6: (5, mate)}

    def obs_copy(slot, i):
        source, peer = routes[slot]
        run = pl.ds(i * cut, cut)
        src = observed.at[run] if source == 0 else obs.at[source, run]
        return remote(src, obs.at[slot, run], obs_send.at[slot, i], obs_recv.at[slot, i], peer)

    def sol_copy(slot, c):
        source, peer = routes[slot]
        src = solved.at[:, pl.ds(c * span, span)] if source == 0 else sol.at[c, pl.ds(source * width, width)]
        return remote(src, sol.at[c, pl.ds(slot * width, width)], sol_send.at[slot, c], sol_recv.at[slot, c], peer)

    obs_copies = {(slot, i): obs_copy(slot, i) for slot in routes for i in range(CUTS)}
    sol_copies = {(slot, c): sol_copy(slot, c) for slot in routes for c in range(PARTS)}

    for i in range(CUTS):
        for slot in (2, 4, 1):
            obs_copies[slot, i].start()
    for c in range(PARTS):
        sol_copies[2, c].start()

    scale = 1.0 / (members - 1)
    levels = [table[i] * scale for i in range(table.shape[0])]

    def find_rho(slot):
        index_loads[slot].wait()

        def body(i, carry):
            run = pl.ds(pl.multiple_of(i * 64, 64), 64)
            at = index[slot, run, :]
            values = levels
            bit = 1
            while len(values) > 1:
                odd = (at & bit) != 0
                values = [jnp.where(odd, values[k + 1], values[k]) for k in range(0, len(values), 2)]
                bit *= 2
            rho[slot, run, :] = values[0]
            return carry

        lax.fori_loop(0, rows // 64, body, 0)

    def weigh(slot):
        block = obs.at[slot]

        def body(i, carry):
            run = pl.ds(pl.multiple_of(i * 256, 256), 256)
            cov = lax.dot_general(
                x_half[run, :], block[...], (((1,), (1,)), ((), ())), preferred_element_type=F32
            )
            weighted[run, slot * width : (slot + 1) * width] = (rho[slot, run, :] * cov).astype(BF16)
            return carry

        lax.fori_loop(0, rows // 256, body, 0)

    def obs_came(slot):
        for i in range(CUTS):
            obs_copies[slot, i].wait_recv()

    for i in range(4):
        loads[i].wait()

        def convert(j, carry):
            run = pl.ds(pl.multiple_of(i * step + j * 16, 16), 16)
            x_half[run, :] = x_full[run, :].astype(BF16)
            return carry

        lax.fori_loop(0, step // 16, convert, 0)
    find_rho(0)
    own_obs.wait()
    weigh(0)
    for i in range(CUTS):
        obs_copies[2, i].wait_recv()
        obs_copies[5, i].start()
        obs_copies[3, i].start()
        if i == 0:
            find_rho(1)
            obs_came(1)
            weigh(1)
            find_rho(4)
    sol_copies[4, 0].start()
    sol_copies[1, 0].start()
    find_rho(2)
    weigh(2)
    obs_came(4)
    weigh(4)
    sol_copies[2, 0].wait_recv()
    sol_copies[5, 0].start()
    sol_copies[3, 0].start()
    find_rho(3)
    find_rho(5)
    obs_copies[5, 0].wait_recv()
    obs_copies[6, 0].start()
    find_rho(6)
    obs_came(3)
    weigh(3)
    for i in range(1, CUTS):
        obs_copies[5, i].wait_recv()
        obs_copies[6, i].start()
    weigh(5)
    for c in range(1, PARTS):
        sol_copies[4, c].start()
        sol_copies[1, c].start()
        sol_copies[2, c].wait_recv()
        sol_copies[5, c].start()
        sol_copies[3, c].start()
    obs_came(6)
    weigh(6)

    def rows_of(half, where):
        return pl.ds(pl.multiple_of((half * ring + where) * share, share), share)

    def y_copy(c, way_y, kind):
        peer = {"y": y_next[way_y]}
        if kind == 0:
            src, dst = part.at[c, rows_of(way_y, far)], passed.at[c, way_y]
        elif kind == 1:
            src, dst = part.at[c, rows_of(1 - way_y, y_next[way_y])], came.at[c, way_y, 1 - way_y]
        else:
            src, dst = joined.at[c, way_y], came.at[c, way_y, way_y]
        return remote(src, dst, y_send.at[c, way_y, kind], y_recv.at[c, way_y, kind], peer)

    y_copies = {(c, w, k): y_copy(c, w, k) for c in range(PARTS) for w in range(2) for k in range(3)}
    x_copies = [
        remote(half_out.at[c], half_in.at[c], x_send.at[c], x_recv.at[c], opposite) for c in range(PARTS)
    ]
    writes = [
        pltpu.make_async_copy(result.at[c], out.at[:, pl.ds(c * span, span)], out_sem.at[c]) for c in range(PARTS)
    ]

    def increments(c):
        def body(i, carry):
            run = pl.ds(pl.multiple_of(i * 256, 256), 256)
            total = jnp.dot(weighted[run, :], sol[c], preferred_element_type=F32)
            part[c, run, :] = total.astype(BF16)
            return carry

        lax.fori_loop(0, rows // 256, body, 0)

    def join(c):
        for w in range(2):
            y_copies[c, w, 0].wait_recv()
            joined[c, w] = (part[c, rows_of(w, y_next[w]), :].astype(F32) + passed[c, w].astype(F32)).astype(BF16)
            y_copies[c, w, 2].start()

    def gather(c):
        for w in range(2):
            for k in (1, 2):
                y_copies[c, w, k].wait_recv()

        def sum_of(half):
            mine = part[c, rows_of(half, y), :].astype(F32)
            return mine + came[c, 0, half].astype(F32) + came[c, 1, half].astype(F32)

        half_out[c] = sum_of(1 - xh).astype(BF16)
        x_copies[c].start()
        half_own[c] = sum_of(xh) + x_full[rows_of(xh, y), c * span : (c + 1) * span]

    def finish(c):
        x_copies[c].wait_recv()
        result[c] = half_own[c] + half_in[c].astype(F32)
        writes[c].start()

    for c in range(PARTS):
        sol_copies[5, c].wait_recv()
        sol_copies[6, c].start()
        own_sol[c].wait()
        for slot in (1, 3, 4, 6):
            sol_copies[slot, c].wait_recv()
        increments(c)
        for k in range(2):
            for w in range(2):
                y_copies[c, w, k].start()
        if c >= 1:
            join(c - 1)
        if c >= 2:
            gather(c - 2)
    join(PARTS - 1)
    for c in range(max(PARTS - 2, 0), PARTS):
        gather(c)
    for c in range(PARTS):
        finish(c)
    for copy in (*obs_copies.values(), *sol_copies.values(), *y_copies.values(), *x_copies):
        copy.wait_send()
    for copy in writes:
        copy.wait()


def per_device(perturb, observed, solved, taper_index, taper_table):
    rows, members = perturb.shape
    width = observed.shape[0]
    ring = lax.axis_size("y")
    share, span = rows // (2 * ring), members // PARTS
    anywhere = pl.BlockSpec(memory_space=pl.ANY)
    dma = pltpu.SemaphoreType.DMA
    return pl.pallas_call(
        kernel,
        out_shape=jax.ShapeDtypeStruct((share, members), F32),
        in_specs=[anywhere] * 4 + [pl.BlockSpec(memory_space=pltpu.SMEM)],
        out_specs=anywhere,
        scratch_shapes=[
            pltpu.VMEM((rows, members), F32),
            pltpu.VMEM((rows, members), BF16),
            pltpu.VMEM((SLOTS, width, members), BF16),
            pltpu.VMEM((PARTS, SLOTS * width, span), BF16),
            pltpu.VMEM((SLOTS, rows, width), jnp.int32),
            pltpu.VMEM((SLOTS, rows, width), F32),
            pltpu.VMEM((rows, SLOTS * width), BF16),
            pltpu.VMEM((PARTS, rows, span), BF16),
            pltpu.VMEM((PARTS, 2, share, span), BF16),
            pltpu.VMEM((PARTS, 2, share, span), BF16),
            pltpu.VMEM((PARTS, 2, 2, share, span), BF16),
            pltpu.VMEM((PARTS, share, span), BF16),
            pltpu.VMEM((PARTS, share, span), BF16),
            pltpu.VMEM((PARTS, share, span), F32),
            pltpu.VMEM((PARTS, share, span), F32),
            dma((4,)),
            dma,
            dma((PARTS,)),
            dma((SLOTS,)),
            dma((PARTS,)),
            dma((SLOTS, CUTS)),
            dma((SLOTS, CUTS)),
            dma((SLOTS, PARTS)),
            dma((SLOTS, PARTS)),
            dma((PARTS, 2, 3)),
            dma((PARTS, 2, 3)),
            dma((PARTS,)),
            dma((PARTS,)),
        ],
        compiler_params=pltpu.CompilerParams(
            collective_id=0, has_side_effects=True, vmem_limit_bytes=48 * 1024 * 1024
        ),
        name="tile_update",
    )(perturb, observed, solved, taper_index, taper_table)


AXES = ("z", "xl", "core", "xh", "y")


def solution(mesh):
    lon, obs = mesh.shape["lon"], mesh.shape["obs"]
    torus = Mesh(mesh.devices.reshape(lon // 4, 2, 2, 2, obs // 2), AXES)
    near, group = AXES[:3], AXES[3:]
    in_specs = (P(near, None), P(AXES, None), P(AXES, None), P(near, group), P())
    return jax.shard_map(
        per_device, mesh=torus, in_specs=in_specs, out_specs=P(AXES, None), check_vma=False
    )
```

```python
import functools

import jax
import jax.numpy as jnp
from jax import lax
from jax.experimental import pallas as pl
from jax.experimental.pallas import tpu as pltpu
from jax.sharding import Mesh
from jax.sharding import PartitionSpec as P

MESH = pl.DeviceIdType.MESH
BF16, F32 = jnp.bfloat16, jnp.float32
SLOTS = 7
CUTS = 2
TILE = 256
PARTS = 4
OUTER = (0, 1, 2, 3, -3, -2, -1)
INNER = (0, -1, 2, 1, 3, -2, -3)


def kernel(
    perturb, observed, solved, taper_index, table, out,
    x_full, x_half, obs, sol, index, rho, weighted, part, passed, joined, came, half_out, half_in, half_own, result,
    load_sem, obs_load_sem, sol_load_sem, index_sem, out_sem,
    obs_send, obs_recv, sol_send, sol_recv, y_send, y_recv, x_send, x_recv,
):
    z, xl, core, xh, y = (lax.axis_index(a) for a in ("z", "xl", "core", "xh", "y"))
    depth, ring = lax.axis_size("z"), lax.axis_size("y")
    rows, members = perturb.shape
    width = observed.shape[0]
    cut = width // CUTS
    span = members // PARTS
    share = rows // (2 * ring)
    way = 1 - 2 * xl
    side = 2 * core - 1
    inner = xl + core - 2 * xl * core

    mate = {"core": 1 - core}
    across = {"xl": 1 - xl}
    slant = {"z": lax.rem(z + side + depth, depth), "core": 1 - core}
    ahead = {"z": lax.rem(z + way + depth, depth)}
    behind = {"z": lax.rem(z - way + depth, depth)}
    y_up, y_down = lax.rem(y + 1, ring), lax.rem(y + ring - 1, ring)
    far = lax.rem(y + 2, ring)
    y_next = (y_up, y_down)
    opposite = {"xh": 1 - xh}

    step = rows // 4
    loads = [
        pltpu.make_async_copy(perturb.at[pl.ds(i * step, step)], x_full.at[pl.ds(i * step, step)], load_sem.at[i])
        for i in range(4)
    ]
    own_obs = pltpu.make_async_copy(observed, obs.at[pl.ds(0, width)], obs_load_sem)
    own_sol = [
        pltpu.make_async_copy(solved.at[:, pl.ds(c * span, span)], sol.at[c, pl.ds(0, width)], sol_load_sem.at[c])
        for c in range(PARTS)
    ]
    index_loads = []
    for slot in range(SLOTS):
        offset = way * (OUTER[slot] + inner * (INNER[slot] - OUTER[slot]))
        start = pl.multiple_of((offset + SLOTS // 2) * width, width)
        index_loads.append(
            pltpu.make_async_copy(taper_index.at[:, pl.ds(start, width)], index.at[slot], index_sem.at[slot])
        )

    barrier = pltpu.get_barrier_semaphore()
    peers = (mate, across, slant, ahead, behind, {"y": y_up}, {"y": y_down}, opposite)
    for peer in peers:
        pl.semaphore_signal(barrier, inc=1, device_id=peer, device_id_type=MESH)
    own_obs.start()
    for i in range(4):
        loads[i].start()
    for slot in (0, 1, 4, 2, 3, 5, 6):
        index_loads[slot].start()
    for c in range(PARTS):
        own_sol[c].start()
    pl.semaphore_wait(barrier, len(peers))

    def remote(src, dst, send, recv, peer):
        return pltpu.make_async_remote_copy(
            src_ref=src, dst_ref=dst, send_sem=send, recv_sem=recv, device_id=peer, device_id_type=MESH
        )

    routes = {1: (0, mate), 2: (0, across), 4: (0, slant), 5: (2, ahead), 3: (2, mate), 6: (5, mate)}

    def obs_copy(slot, i):
        source, peer = routes[slot]
        src = observed.at[pl.ds(i * cut, cut)] if source == 0 else obs.at[pl.ds(source * width + i * cut, cut)]
        return remote(src, obs.at[pl.ds(slot * width + i * cut, cut)], obs_send.at[slot, i], obs_recv.at[slot, i], peer)

    def sol_copy(slot, c):
        source, peer = routes[slot]
        src = solved.at[:, pl.ds(c * span, span)] if source == 0 else sol.at[c, pl.ds(source * width, width)]
        return remote(src, sol.at[c, pl.ds(slot * width, width)], sol_send.at[slot, c], sol_recv.at[slot, c], peer)

    obs_copies = {(slot, i): obs_copy(slot, i) for slot in routes for i in range(CUTS)}
    sol_copies = {(slot, c): sol_copy(slot, c) for slot in routes for c in range(PARTS)}

    for i in range(CUTS):
        for slot in (2, 4, 1):
            obs_copies[slot, i].start()
    for c in range(PARTS):
        sol_copies[2, c].start()

    def find_rho(slot):
        index_loads[slot].wait()
        values = jnp.broadcast_to(table[...], (64, width))

        def body(i, carry):
            run = pl.ds(pl.multiple_of(i * 64, 64), 64)
            rho[run, slot * width : (slot + 1) * width] = jnp.take_along_axis(values, index[slot, run, :], axis=1)
            return carry

        lax.fori_loop(0, rows // 64, body, 0)

    def weigh(first, count):
        columns = slice(first * width, (first + count) * width)

        def body(i, carry):
            run = pl.ds(pl.multiple_of(i * TILE, TILE), TILE)
            cov = lax.dot_general(
                x_half[run, :], obs[columns, :], (((1,), (1,)), ((), ())), preferred_element_type=F32
            )
            weighted[run, columns] = (rho[run, columns] * cov).astype(BF16)
            return carry

        lax.fori_loop(0, rows // TILE, body, 0)

    def obs_came(slot):
        for i in range(CUTS):
            obs_copies[slot, i].wait_recv()

    for i in range(4):
        loads[i].wait()

        def convert(j, carry):
            run = pl.ds(pl.multiple_of(i * step + j * 16, 16), 16)
            x_half[run, :] = x_full[run, :].astype(BF16)
            return carry

        lax.fori_loop(0, step // 16, convert, 0)
    def pass_obs(slot_from, i):
        obs_copies[slot_from, i].wait_recv()
        for slot, (source, _) in routes.items():
            if source == slot_from:
                obs_copies[slot, i].start()

    def send_sol(c):
        sol_copies[4, c].start()
        sol_copies[1, c].start()

    def pass_sol(slot_from, c):
        sol_copies[slot_from, c].wait_recv()
        for slot, (source, _) in routes.items():
            if source == slot_from:
                sol_copies[slot, c].start()

    find_rho(0)
    find_rho(1)
    own_obs.wait()
    obs_came(1)
    weigh(0, 2)
    pass_obs(2, 0)
    find_rho(4)
    obs_came(4)
    weigh(4, 1)
    pass_obs(2, 1)
    send_sol(0)
    find_rho(2)
    find_rho(3)
    obs_came(3)
    weigh(2, 2)
    pass_sol(2, 0)
    send_sol(1)
    find_rho(5)
    find_rho(6)
    pass_obs(5, 0)
    pass_sol(2, 1)
    send_sol(2)
    pass_obs(5, 1)
    obs_came(6)
    weigh(5, 2)
    pass_sol(2, 2)
    send_sol(3)

    def rows_of(half, where):
        return pl.ds(pl.multiple_of((half * ring + where) * share, share), share)

    def y_copy(c, way_y, kind):
        peer = {"y": y_next[way_y]}
        if kind == 0:
            src, dst = part.at[c, rows_of(way_y, far)], passed.at[c, way_y]
        elif kind == 1:
            src, dst = part.at[c, rows_of(1 - way_y, y_next[way_y])], came.at[c, way_y, 1 - way_y]
        else:
            src, dst = joined.at[c, way_y], came.at[c, way_y, way_y]
        return remote(src, dst, y_send.at[c, way_y, kind], y_recv.at[c, way_y, kind], peer)

    y_copies = {(c, w, k): y_copy(c, w, k) for c in range(PARTS) for w in range(2) for k in range(3)}
    x_copies = [
        remote(half_out.at[c], half_in.at[c], x_send.at[c], x_recv.at[c], opposite) for c in range(PARTS)
    ]
    writes = [
        pltpu.make_async_copy(result.at[c], out.at[:, pl.ds(c * span, span)], out_sem.at[c]) for c in range(PARTS)
    ]

    def increments(c):
        def body(i, carry):
            run = pl.ds(pl.multiple_of(i * 256, 256), 256)
            total = jnp.dot(weighted[run, :], sol[c], preferred_element_type=F32)
            part[c, run, :] = total.astype(BF16)
            return carry

        lax.fori_loop(0, rows // 256, body, 0)

    def join(c):
        for w in range(2):
            y_copies[c, w, 0].wait_recv()
            joined[c, w] = (part[c, rows_of(w, y_next[w]), :].astype(F32) + passed[c, w].astype(F32)).astype(BF16)
            y_copies[c, w, 2].start()

    def gather(c):
        for w in range(2):
            for k in (1, 2):
                y_copies[c, w, k].wait_recv()

        def sum_of(half):
            mine = part[c, rows_of(half, y), :].astype(F32)
            return mine + came[c, 0, half].astype(F32) + came[c, 1, half].astype(F32)

        half_out[c] = sum_of(1 - xh).astype(BF16)
        x_copies[c].start()
        half_own[c] = sum_of(xh) + x_full[rows_of(xh, y), c * span : (c + 1) * span]

    def finish(c):
        x_copies[c].wait_recv()
        result[c] = half_own[c] + half_in[c].astype(F32)
        writes[c].start()

    for c in range(PARTS):
        pass_sol(5, c)
        own_sol[c].wait()
        for slot in (1, 3, 4, 6):
            sol_copies[slot, c].wait_recv()
        increments(c)
        for k in range(2):
            for w in range(2):
                y_copies[c, w, k].start()
        if c == 0:
            pass_sol(2, 3)
        if c >= 1:
            join(c - 1)
        if c >= 2:
            gather(c - 2)
    join(PARTS - 1)
    for c in range(max(PARTS - 2, 0), PARTS):
        gather(c)
    for c in range(PARTS):
        finish(c)
    for copy in (*obs_copies.values(), *sol_copies.values(), *y_copies.values(), *x_copies):
        copy.wait_send()
    for copy in writes:
        copy.wait()


def per_device(perturb, observed, solved, taper_index, taper_table):
    rows, members = perturb.shape
    width = observed.shape[0]
    ring = lax.axis_size("y")
    share, span = rows // (2 * ring), members // PARTS
    levels = jnp.pad(taper_table, (0, width - taper_table.shape[0])) / (members - 1)
    levels = levels.reshape(1, width)
    anywhere = pl.BlockSpec(memory_space=pl.ANY)
    dma = pltpu.SemaphoreType.DMA
    return pl.pallas_call(
        kernel,
        out_shape=jax.ShapeDtypeStruct((share, members), F32),
        in_specs=[anywhere] * 4 + [pl.BlockSpec(memory_space=pltpu.VMEM)],
        out_specs=anywhere,
        scratch_shapes=[
            pltpu.VMEM((rows, members), F32),
            pltpu.VMEM((rows, members), BF16),
            pltpu.VMEM((SLOTS * width, members), BF16),
            pltpu.VMEM((PARTS, SLOTS * width, span), BF16),
            pltpu.VMEM((SLOTS, rows, width), jnp.int32),
            pltpu.VMEM((rows, SLOTS * width), F32),
            pltpu.VMEM((rows, SLOTS * width), BF16),
            pltpu.VMEM((PARTS, rows, span), BF16),
            pltpu.VMEM((PARTS, 2, share, span), BF16),
            pltpu.VMEM((PARTS, 2, share, span), BF16),
            pltpu.VMEM((PARTS, 2, 2, share, span), BF16),
            pltpu.VMEM((PARTS, share, span), BF16),
            pltpu.VMEM((PARTS, share, span), BF16),
            pltpu.VMEM((PARTS, share, span), F32),
            pltpu.VMEM((PARTS, share, span), F32),
            dma((4,)),
            dma,
            dma((PARTS,)),
            dma((SLOTS,)),
            dma((PARTS,)),
            dma((SLOTS, CUTS)),
            dma((SLOTS, CUTS)),
            dma((SLOTS, PARTS)),
            dma((SLOTS, PARTS)),
            dma((PARTS, 2, 3)),
            dma((PARTS, 2, 3)),
            dma((PARTS,)),
            dma((PARTS,)),
        ],
        compiler_params=pltpu.CompilerParams(
            collective_id=0, has_side_effects=True, vmem_limit_bytes=67_000_000
        ),
        name="tile_update",
    )(perturb, observed, solved, taper_index, levels)


AXES = ("z", "xl", "core", "xh", "y")


def solution(mesh):
    lon, obs = mesh.shape["lon"], mesh.shape["obs"]
    torus = Mesh(mesh.devices.reshape(lon // 4, 2, 2, 2, obs // 2), AXES)
    near, group = AXES[:3], AXES[3:]
    in_specs = (P(near, None), P(AXES, None), P(AXES, None), P(near, group), P())
    return jax.shard_map(
        per_device, mesh=torus, in_specs=in_specs, out_specs=P(AXES, None), check_vma=False
    )
```

```python
import functools

import jax
import jax.numpy as jnp
from jax import lax
from jax.experimental import pallas as pl
from jax.experimental.pallas import tpu as pltpu
from jax.sharding import Mesh
from jax.sharding import PartitionSpec as P

MESH = pl.DeviceIdType.MESH
BF16, F32 = jnp.bfloat16, jnp.float32
SLOTS = 7
CUTS = 4
LEAD = 3
TILE = 256
PARTS = 4
OUTER = (0, 1, 2, 3, -3, -2, -1)
INNER = (0, -1, 2, 1, 3, -2, -3)


def kernel(
    perturb, observed, solved, taper_index, table, out,
    x_full, x_half, obs, sol, index, rho, weighted, part, passed, joined, came, half_out, half_in, half_own, result,
    load_sem, obs_load_sem, sol_load_sem, index_sem, out_sem,
    obs_send, obs_recv, sol_send, sol_recv, y_send, y_recv, x_send, x_recv,
):
    z, xl, core, xh, y = (lax.axis_index(a) for a in ("z", "xl", "core", "xh", "y"))
    depth, ring = lax.axis_size("z"), lax.axis_size("y")
    rows, members = perturb.shape
    width = observed.shape[0]
    cut = width // CUTS
    span = members // PARTS
    share = rows // (2 * ring)
    way = 1 - 2 * xl
    side = 2 * core - 1
    inner = xl + core - 2 * xl * core

    mate = {"core": 1 - core}
    across = {"xl": 1 - xl}
    slant = {"z": lax.rem(z + side + depth, depth), "core": 1 - core}
    ahead = {"z": lax.rem(z + way + depth, depth)}
    behind = {"z": lax.rem(z - way + depth, depth)}
    y_up, y_down = lax.rem(y + 1, ring), lax.rem(y + ring - 1, ring)
    far = lax.rem(y + 2, ring)
    y_next = (y_up, y_down)
    opposite = {"xh": 1 - xh}

    step = rows // 4
    loads = [
        pltpu.make_async_copy(perturb.at[pl.ds(i * step, step)], x_full.at[pl.ds(i * step, step)], load_sem.at[i])
        for i in range(4)
    ]
    own_obs = pltpu.make_async_copy(observed, obs.at[pl.ds(0, width)], obs_load_sem)
    own_sol = [
        pltpu.make_async_copy(solved.at[:, pl.ds(c * span, span)], sol.at[c, pl.ds(0, width)], sol_load_sem.at[c])
        for c in range(PARTS)
    ]
    index_loads = []
    for slot in range(SLOTS):
        offset = way * (OUTER[slot] + inner * (INNER[slot] - OUTER[slot]))
        start = pl.multiple_of((offset + SLOTS // 2) * width, width)
        index_loads.append(
            pltpu.make_async_copy(taper_index.at[:, pl.ds(start, width)], index.at[slot], index_sem.at[slot])
        )

    barrier = pltpu.get_barrier_semaphore()
    peers = (mate, across, slant, ahead, behind, {"y": y_up}, {"y": y_down}, opposite)
    for peer in peers:
        pl.semaphore_signal(barrier, inc=1, device_id=peer, device_id_type=MESH)
    own_obs.start()
    for c in range(PARTS):
        own_sol[c].start()
    for i in range(4):
        loads[i].start()
    for slot in (0, 1, 4, 2, 3, 5, 6):
        index_loads[slot].start()
    pl.semaphore_wait(barrier, len(peers))

    def remote(src, dst, send, recv, peer):
        return pltpu.make_async_remote_copy(
            src_ref=src, dst_ref=dst, send_sem=send, recv_sem=recv, device_id=peer, device_id_type=MESH
        )

    routes = {1: (0, mate), 2: (0, across), 4: (0, slant), 5: (2, ahead), 3: (2, mate), 6: (5, mate)}

    def obs_copy(slot, i):
        source, peer = routes[slot]
        src = observed.at[pl.ds(i * cut, cut)] if source == 0 else obs.at[pl.ds(source * width + i * cut, cut)]
        return remote(src, obs.at[pl.ds(slot * width + i * cut, cut)], obs_send.at[slot, i], obs_recv.at[slot, i], peer)

    def sol_copy(slot, c):
        source, peer = routes[slot]
        src = sol.at[c, pl.ds(source * width, width)]
        return remote(src, sol.at[c, pl.ds(slot * width, width)], sol_send.at[slot, c], sol_recv.at[slot, c], peer)

    obs_copies = {(slot, i): obs_copy(slot, i) for slot in routes for i in range(CUTS)}
    sol_copies = {(slot, c): sol_copy(slot, c) for slot in routes for c in range(PARTS)}

    for i in range(CUTS):
        for slot in (2, 4, 1):
            obs_copies[slot, i].start()
    for c in range(PARTS):
        own_sol[c].wait()
        sol_copies[2, c].start()

    levels = [table[i] * (1.0 / (members - 1)) for i in range(table.shape[0])]

    def find_rho(slot):
        index_loads[slot].wait()

        def body(i, carry):
            run = pl.ds(pl.multiple_of(i * 64, 64), 64)
            at = index[slot, run, :]
            values, bit = levels, 1
            while len(values) > 1:
                odd = (at & bit) != 0
                values = [jnp.where(odd, values[k + 1], values[k]) for k in range(0, len(values), 2)]
                bit *= 2
            rho[run, slot * width : (slot + 1) * width] = values[0]
            return carry

        lax.fori_loop(0, rows // 64, body, 0)

    def weigh(first, count):
        columns = slice(first * width, (first + count) * width)

        def body(i, carry):
            run = pl.ds(pl.multiple_of(i * TILE, TILE), TILE)
            cov = lax.dot_general(
                x_half[run, :], obs[columns, :], (((1,), (1,)), ((), ())), preferred_element_type=F32
            )
            weighted[run, columns] = (rho[run, columns] * cov).astype(BF16)
            return carry

        lax.fori_loop(0, rows // TILE, body, 0)

    def obs_came(slot):
        for i in range(CUTS):
            obs_copies[slot, i].wait_recv()

    for i in range(4):
        loads[i].wait()

        def convert(j, carry):
            run = pl.ds(pl.multiple_of(i * step + j * 16, 16), 16)
            x_half[run, :] = x_full[run, :].astype(BF16)
            return carry

        lax.fori_loop(0, step // 16, convert, 0)
    def pass_obs(slot_from, i):
        obs_copies[slot_from, i].wait_recv()
        for slot, (source, _) in routes.items():
            if source == slot_from:
                obs_copies[slot, i].start()

    def send_sol(c):
        sol_copies[4, c].start()
        sol_copies[1, c].start()

    def pass_sol(slot_from, c):
        sol_copies[slot_from, c].wait_recv()
        for slot, (source, _) in routes.items():
            if source == slot_from:
                sol_copies[slot, c].start()

    def sol_step(c):
        send_sol(c)
        pass_sol(2, c)

    find_rho(0)
    find_rho(1)
    own_obs.wait()
    obs_came(1)
    weigh(0, 2)
    for i in range(CUTS // 2):
        pass_obs(2, i)
    find_rho(4)
    obs_came(4)
    weigh(4, 1)
    for i in range(CUTS // 2, CUTS):
        pass_obs(2, i)
    find_rho(2)
    find_rho(3)
    obs_came(3)
    weigh(2, 2)
    sol_step(0)
    find_rho(5)
    find_rho(6)
    for i in range(CUTS - 1):
        pass_obs(5, i)
    sol_step(1)
    pass_obs(5, CUTS - 1)
    obs_came(6)
    weigh(5, 2)
    for c in range(2, LEAD):
        sol_step(c)

    def rows_of(half, where):
        return pl.ds(pl.multiple_of((half * ring + where) * share, share), share)

    def y_copy(c, way_y, kind):
        peer = {"y": y_next[way_y]}
        if kind == 0:
            src, dst = part.at[c, rows_of(way_y, far)], passed.at[c, way_y]
        elif kind == 1:
            src, dst = part.at[c, rows_of(1 - way_y, y_next[way_y])], came.at[c, way_y, 1 - way_y]
        else:
            src, dst = joined.at[c, way_y], came.at[c, way_y, way_y]
        return remote(src, dst, y_send.at[c, way_y, kind], y_recv.at[c, way_y, kind], peer)

    y_copies = {(c, w, k): y_copy(c, w, k) for c in range(PARTS) for w in range(2) for k in range(3)}
    x_copies = [
        remote(half_out.at[c], half_in.at[c], x_send.at[c], x_recv.at[c], opposite) for c in range(PARTS)
    ]
    writes = [
        pltpu.make_async_copy(result.at[c], out.at[:, pl.ds(c * span, span)], out_sem.at[c]) for c in range(PARTS)
    ]

    def increments(c):
        def body(i, carry):
            run = pl.ds(pl.multiple_of(i * 256, 256), 256)
            total = jnp.dot(weighted[run, :], sol[c], preferred_element_type=F32)
            part[c, run, :] = total.astype(BF16)
            return carry

        lax.fori_loop(0, rows // 256, body, 0)

    def join(c):
        for w in range(2):
            y_copies[c, w, 0].wait_recv()
            joined[c, w] = (part[c, rows_of(w, y_next[w]), :].astype(F32) + passed[c, w].astype(F32)).astype(BF16)
            y_copies[c, w, 2].start()

    def gather(c):
        for w in range(2):
            for k in (1, 2):
                y_copies[c, w, k].wait_recv()

        def sum_of(half):
            mine = part[c, rows_of(half, y), :].astype(F32)
            return mine + came[c, 0, half].astype(F32) + came[c, 1, half].astype(F32)

        half_out[c] = sum_of(1 - xh).astype(BF16)
        x_copies[c].start()
        half_own[c] = sum_of(xh) + x_full[rows_of(xh, y), c * span : (c + 1) * span]

    def finish(c):
        x_copies[c].wait_recv()
        result[c] = half_own[c] + half_in[c].astype(F32)
        writes[c].start()

    for c in range(PARTS):
        pass_sol(5, c)
        for slot in (1, 3, 4, 6):
            sol_copies[slot, c].wait_recv()
        increments(c)
        for k in range(2):
            for w in range(2):
                y_copies[c, w, k].start()
        if c + LEAD < PARTS:
            sol_step(c + LEAD)
        if c >= 1:
            join(c - 1)
        if c >= 2:
            gather(c - 2)
    join(PARTS - 1)
    for c in range(max(PARTS - 2, 0), PARTS):
        gather(c)
    for c in range(PARTS):
        finish(c)
    for copy in (*obs_copies.values(), *sol_copies.values(), *y_copies.values(), *x_copies):
        copy.wait_send()
    for copy in writes:
        copy.wait()


def per_device(perturb, observed, solved, taper_index, taper_table):
    rows, members = perturb.shape
    width = observed.shape[0]
    ring = lax.axis_size("y")
    share, span = rows // (2 * ring), members // PARTS
    anywhere = pl.BlockSpec(memory_space=pl.ANY)
    dma = pltpu.SemaphoreType.DMA
    return pl.pallas_call(
        kernel,
        out_shape=jax.ShapeDtypeStruct((share, members), F32),
        in_specs=[anywhere] * 4 + [pl.BlockSpec(memory_space=pltpu.SMEM)],
        out_specs=anywhere,
        scratch_shapes=[
            pltpu.VMEM((rows, members), F32),
            pltpu.VMEM((rows, members), BF16),
            pltpu.VMEM((SLOTS * width, members), BF16),
            pltpu.VMEM((PARTS, SLOTS * width, span), BF16),
            pltpu.VMEM((SLOTS, rows, width), jnp.int32),
            pltpu.VMEM((rows, SLOTS * width), F32),
            pltpu.VMEM((rows, SLOTS * width), BF16),
            pltpu.VMEM((PARTS, rows, span), BF16),
            pltpu.VMEM((PARTS, 2, share, span), BF16),
            pltpu.VMEM((PARTS, 2, share, span), BF16),
            pltpu.VMEM((PARTS, 2, 2, share, span), BF16),
            pltpu.VMEM((PARTS, share, span), BF16),
            pltpu.VMEM((PARTS, share, span), BF16),
            pltpu.VMEM((PARTS, share, span), F32),
            pltpu.VMEM((PARTS, share, span), F32),
            dma((4,)),
            dma,
            dma((PARTS,)),
            dma((SLOTS,)),
            dma((PARTS,)),
            dma((SLOTS, CUTS)),
            dma((SLOTS, CUTS)),
            dma((SLOTS, PARTS)),
            dma((SLOTS, PARTS)),
            dma((PARTS, 2, 3)),
            dma((PARTS, 2, 3)),
            dma((PARTS,)),
            dma((PARTS,)),
        ],
        compiler_params=pltpu.CompilerParams(
            collective_id=0, has_side_effects=True, vmem_limit_bytes=50_000_000
        ),
        name="tile_update",
    )(*(pltpu.with_memory_space_constraint(a, pltpu.HBM) for a in (perturb, observed, solved, taper_index, taper_table)))


AXES = ("z", "xl", "core", "xh", "y")


def solution(mesh):
    lon, obs = mesh.shape["lon"], mesh.shape["obs"]
    torus = Mesh(mesh.devices.reshape(lon // 4, 2, 2, 2, obs // 2), AXES)
    near, group = AXES[:3], AXES[3:]
    in_specs = (P(near, None), P(AXES, None), P(AXES, None), P(near, group), P())
    return jax.shard_map(
        per_device, mesh=torus, in_specs=in_specs, out_specs=P(AXES, None), check_vma=False
    )
```

```python
import functools

import jax
import jax.numpy as jnp
from jax import lax
from jax.experimental import pallas as pl
from jax.experimental.pallas import tpu as pltpu
from jax.sharding import Mesh
from jax.sharding import PartitionSpec as P

MESH = pl.DeviceIdType.MESH
BF16, F32 = jnp.bfloat16, jnp.float32
SLOTS = 7
CUTS = 4
RING_FIRST, ACROSS_FIRST = (1, 3), (0, 2)
LEAD = 3
TILE = 256
PARTS = 4
OUTER = (0, 1, 2, 3, -3, -2, -1)
INNER = (0, -1, 2, 1, 3, -2, -3)


def kernel(
    perturb, observed, solved, taper_index, table, out,
    x_full, x_half, obs, sol, index, rho, weighted, part, passed, joined, came, half_out, half_in, half_own, result,
    cross_in, cross_sum, ring_in,
    load_sem, obs_load_sem, sol_load_sem, index_sem, out_sem,
    obs_send, obs_recv, sol_send, sol_recv, y_send, y_recv, x_send, x_recv,
    cross_send, cross_recv, ring_send, ring_recv,
):
    z, xl, core, xh, y = (lax.axis_index(a) for a in ("z", "xl", "core", "xh", "y"))
    depth, ring = lax.axis_size("z"), lax.axis_size("y")
    rows, members = perturb.shape
    width = observed.shape[0]
    cut = width // CUTS
    span = members // PARTS
    share = rows // (2 * ring)
    way = 1 - 2 * xl
    side = 2 * core - 1
    inner = xl + core - 2 * xl * core

    mate = {"core": 1 - core}
    across = {"xl": 1 - xl}
    slant = {"z": lax.rem(z + side + depth, depth), "core": 1 - core}
    ahead = {"z": lax.rem(z + way + depth, depth)}
    behind = {"z": lax.rem(z - way + depth, depth)}
    y_up, y_down = lax.rem(y + 1, ring), lax.rem(y + ring - 1, ring)
    far = lax.rem(y + 2, ring)
    y_next = (y_up, y_down)
    opposite = {"xh": 1 - xh}

    step = rows // 4
    loads = [
        pltpu.make_async_copy(perturb.at[pl.ds(i * step, step)], x_full.at[pl.ds(i * step, step)], load_sem.at[i])
        for i in range(4)
    ]
    own_obs = pltpu.make_async_copy(observed, obs.at[pl.ds(0, width)], obs_load_sem)
    own_sol = [
        pltpu.make_async_copy(solved.at[:, pl.ds(c * span, span)], sol.at[c, pl.ds(0, width)], sol_load_sem.at[c])
        for c in range(PARTS)
    ]
    index_loads = []
    for slot in range(SLOTS):
        offset = way * (OUTER[slot] + inner * (INNER[slot] - OUTER[slot]))
        start = pl.multiple_of((offset + SLOTS // 2) * width, width)
        index_loads.append(
            pltpu.make_async_copy(taper_index.at[:, pl.ds(start, width)], index.at[slot], index_sem.at[slot])
        )

    barrier = pltpu.get_barrier_semaphore()
    peers = (mate, across, slant, ahead, behind, {"y": y_up}, {"y": y_down}, {"y": far}, opposite)
    for peer in peers:
        pl.semaphore_signal(barrier, inc=1, device_id=peer, device_id_type=MESH)
    own_obs.start()
    for c in range(PARTS):
        own_sol[c].start()
    for i in range(4):
        loads[i].start()
    for slot in (0, 1, 4, 2, 3, 5, 6):
        index_loads[slot].start()
    pl.semaphore_wait(barrier, len(peers))

    def remote(src, dst, send, recv, peer):
        return pltpu.make_async_remote_copy(
            src_ref=src, dst_ref=dst, send_sem=send, recv_sem=recv, device_id=peer, device_id_type=MESH
        )

    routes = {1: (0, mate), 2: (0, across), 4: (0, slant), 5: (2, ahead), 3: (2, mate), 6: (5, mate)}

    def obs_copy(slot, i):
        source, peer = routes[slot]
        src = observed.at[pl.ds(i * cut, cut)] if source == 0 else obs.at[pl.ds(source * width + i * cut, cut)]
        return remote(src, obs.at[pl.ds(slot * width + i * cut, cut)], obs_send.at[slot, i], obs_recv.at[slot, i], peer)

    def sol_copy(slot, c):
        source, peer = routes[slot]
        src = sol.at[c, pl.ds(source * width, width)]
        return remote(src, sol.at[c, pl.ds(slot * width, width)], sol_send.at[slot, c], sol_recv.at[slot, c], peer)

    obs_copies = {(slot, i): obs_copy(slot, i) for slot in routes for i in range(CUTS)}
    sol_copies = {(slot, c): sol_copy(slot, c) for slot in routes for c in range(PARTS)}

    for i in range(CUTS):
        for slot in (2, 4, 1):
            obs_copies[slot, i].start()
    for c in range(PARTS):
        own_sol[c].wait()
        sol_copies[2, c].start()

    levels = [table[i] * (1.0 / (members - 1)) for i in range(table.shape[0])]

    def find_rho(slot):
        index_loads[slot].wait()

        def body(i, carry):
            run = pl.ds(pl.multiple_of(i * 64, 64), 64)
            at = index[slot, run, :]
            values, bit = levels, 1
            while len(values) > 1:
                odd = (at & bit) != 0
                values = [jnp.where(odd, values[k + 1], values[k]) for k in range(0, len(values), 2)]
                bit *= 2
            rho[run, slot * width : (slot + 1) * width] = values[0]
            return carry

        lax.fori_loop(0, rows // 64, body, 0)

    def weigh(first, count):
        columns = slice(first * width, (first + count) * width)

        def body(i, carry):
            run = pl.ds(pl.multiple_of(i * TILE, TILE), TILE)
            cov = lax.dot_general(
                x_half[run, :], obs[columns, :], (((1,), (1,)), ((), ())), preferred_element_type=F32
            )
            weighted[run, columns] = (rho[run, columns] * cov).astype(BF16)
            return carry

        lax.fori_loop(0, rows // TILE, body, 0)

    def obs_came(slot):
        for i in range(CUTS):
            obs_copies[slot, i].wait_recv()

    for i in range(4):
        loads[i].wait()

        def convert(j, carry):
            run = pl.ds(pl.multiple_of(i * step + j * 16, 16), 16)
            x_half[run, :] = x_full[run, :].astype(BF16)
            return carry

        lax.fori_loop(0, step // 16, convert, 0)
    def pass_obs(slot_from, i):
        obs_copies[slot_from, i].wait_recv()
        for slot, (source, _) in routes.items():
            if source == slot_from:
                obs_copies[slot, i].start()

    def send_sol(c):
        sol_copies[4, c].start()
        sol_copies[1, c].start()

    def pass_sol(slot_from, c):
        sol_copies[slot_from, c].wait_recv()
        for slot, (source, _) in routes.items():
            if source == slot_from:
                sol_copies[slot, c].start()

    def sol_step(c):
        send_sol(c)
        pass_sol(2, c)

    find_rho(0)
    find_rho(1)
    own_obs.wait()
    obs_came(1)
    weigh(0, 2)
    for i in range(CUTS // 2):
        pass_obs(2, i)
    find_rho(4)
    obs_came(4)
    weigh(4, 1)
    for i in range(CUTS // 2, CUTS):
        pass_obs(2, i)
    find_rho(2)
    find_rho(3)
    obs_came(3)
    weigh(2, 2)
    sol_step(0)
    find_rho(5)
    find_rho(6)
    for i in range(CUTS - 1):
        pass_obs(5, i)
    sol_step(1)
    pass_obs(5, CUTS - 1)
    obs_came(6)
    weigh(5, 2)
    for c in range(2, LEAD):
        sol_step(c)

    def rows_of(half, where):
        return pl.ds(pl.multiple_of((half * ring + where) * share, share), share)

    def y_copy(c, way_y, kind):
        peer = {"y": y_next[way_y]}
        if kind == 0:
            src, dst = part.at[c, rows_of(way_y, far)], passed.at[c, way_y]
        elif kind == 1:
            src, dst = part.at[c, rows_of(1 - way_y, y_next[way_y])], came.at[c, way_y, 1 - way_y]
        else:
            src, dst = joined.at[c, way_y], came.at[c, way_y, way_y]
        return remote(src, dst, y_send.at[c, way_y, kind], y_recv.at[c, way_y, kind], peer)

    y_copies = {(c, w, k): y_copy(c, w, k) for c in RING_FIRST for w in range(2) for k in range(3)}
    x_copies = {
        c: remote(half_out.at[c], half_in.at[c], x_send.at[c], x_recv.at[c], opposite) for c in RING_FIRST
    }
    writes = [
        pltpu.make_async_copy(result.at[c], out.at[:, pl.ds(c * span, span)], out_sem.at[c]) for c in range(PARTS)
    ]

    def increments(c):
        def body(i, carry):
            run = pl.ds(pl.multiple_of(i * 256, 256), 256)
            total = jnp.dot(weighted[run, :], sol[c], preferred_element_type=F32)
            part[c, run, :] = total.astype(BF16)
            return carry

        lax.fori_loop(0, rows // 256, body, 0)

    def join(c):
        for w in range(2):
            y_copies[c, w, 0].wait_recv()
            joined[c, w] = (part[c, rows_of(w, y_next[w]), :].astype(F32) + passed[c, w].astype(F32)).astype(BF16)
            y_copies[c, w, 2].start()

    def gather(c):
        for w in range(2):
            for k in (1, 2):
                y_copies[c, w, k].wait_recv()

        def sum_of(half):
            mine = part[c, rows_of(half, y), :].astype(F32)
            return mine + came[c, 0, half].astype(F32) + came[c, 1, half].astype(F32)

        half_out[c] = sum_of(1 - xh).astype(BF16)
        x_copies[c].start()
        half_own[c] = sum_of(xh) + x_full[rows_of(xh, y), c * span : (c + 1) * span]

    def finish(c):
        x_copies[c].wait_recv()
        result[c] = half_own[c] + half_in[c].astype(F32)
        writes[c].start()

    places = {k: lax.rem(y + k, ring) for k in (2, 1, 3, 0)}
    cross_copies = {
        (c, k): remote(
            part.at[c, rows_of(1 - xh, places[k])], cross_in.at[c, k], cross_send.at[c, k], cross_recv.at[c, k], opposite
        )
        for c in ACROSS_FIRST
        for k in places
    }
    ring_copies = {
        (c, k): remote(cross_sum.at[c, k], ring_in.at[c, k], ring_send.at[c, k], ring_recv.at[c, k], {"y": places[k]})
        for c in ACROSS_FIRST
        for k in places
        if k
    }

    def pass_cross(c):
        for k in places:
            cross_copies[c, k].wait_recv()
            total = part[c, rows_of(xh, places[k]), :].astype(F32) + cross_in[c, k].astype(F32)
            if k:
                cross_sum[c, k] = total.astype(BF16)
                ring_copies[c, k].start()
            else:
                half_own[c] = total + x_full[rows_of(xh, y), c * span : (c + 1) * span]

    def finish_cross(c):
        total = half_own[c]
        for k in (1, 3, 2):
            ring_copies[c, k].wait_recv()
            total = total + ring_in[c, k].astype(F32)
        result[c] = total
        writes[c].start()

    for c in range(PARTS):
        pass_sol(5, c)
        for slot in (1, 3, 4, 6):
            sol_copies[slot, c].wait_recv()
        increments(c)
        if c in ACROSS_FIRST:
            for k in places:
                cross_copies[c, k].start()
        else:
            for k in range(2):
                for w in range(2):
                    y_copies[c, w, k].start()
        if c + LEAD < PARTS:
            sol_step(c + LEAD)
        if c == 2:
            join(1)
    pass_cross(0)
    join(3)
    gather(1)
    pass_cross(2)
    gather(3)
    finish_cross(0)
    finish(1)
    finish_cross(2)
    finish(3)
    for copy in (*obs_copies.values(), *sol_copies.values(), *y_copies.values(), *x_copies.values(),
                 *cross_copies.values(), *ring_copies.values()):
        copy.wait_send()
    for copy in writes:
        copy.wait()


def per_device(perturb, observed, solved, taper_index, taper_table):
    rows, members = perturb.shape
    width = observed.shape[0]
    ring = lax.axis_size("y")
    share, span = rows // (2 * ring), members // PARTS
    anywhere = pl.BlockSpec(memory_space=pl.ANY)
    dma = pltpu.SemaphoreType.DMA
    return pl.pallas_call(
        kernel,
        out_shape=jax.ShapeDtypeStruct((share, members), F32),
        in_specs=[anywhere] * 4 + [pl.BlockSpec(memory_space=pltpu.SMEM)],
        out_specs=anywhere,
        scratch_shapes=[
            pltpu.VMEM((rows, members), F32),
            pltpu.VMEM((rows, members), BF16),
            pltpu.VMEM((SLOTS * width, members), BF16),
            pltpu.VMEM((PARTS, SLOTS * width, span), BF16),
            pltpu.VMEM((SLOTS, rows, width), jnp.int32),
            pltpu.VMEM((rows, SLOTS * width), F32),
            pltpu.VMEM((rows, SLOTS * width), BF16),
            pltpu.VMEM((PARTS, rows, span), BF16),
            pltpu.VMEM((PARTS, 2, share, span), BF16),
            pltpu.VMEM((PARTS, 2, share, span), BF16),
            pltpu.VMEM((PARTS, 2, 2, share, span), BF16),
            pltpu.VMEM((PARTS, share, span), BF16),
            pltpu.VMEM((PARTS, share, span), BF16),
            pltpu.VMEM((PARTS, share, span), F32),
            pltpu.VMEM((PARTS, share, span), F32),
            pltpu.VMEM((PARTS, ring, share, span), BF16),
            pltpu.VMEM((PARTS, ring, share, span), BF16),
            pltpu.VMEM((PARTS, ring, share, span), BF16),
            dma((4,)),
            dma,
            dma((PARTS,)),
            dma((SLOTS,)),
            dma((PARTS,)),
            dma((SLOTS, CUTS)),
            dma((SLOTS, CUTS)),
            dma((SLOTS, PARTS)),
            dma((SLOTS, PARTS)),
            dma((PARTS, 2, 3)),
            dma((PARTS, 2, 3)),
            dma((PARTS,)),
            dma((PARTS,)),
            dma((PARTS, ring)),
            dma((PARTS, ring)),
            dma((PARTS, ring)),
            dma((PARTS, ring)),
        ],
        compiler_params=pltpu.CompilerParams(
            collective_id=0, has_side_effects=True, vmem_limit_bytes=50_000_000
        ),
        name="tile_update",
    )(*(pltpu.with_memory_space_constraint(a, pltpu.HBM) for a in (perturb, observed, solved, taper_index, taper_table)))


AXES = ("z", "xl", "core", "xh", "y")


def solution(mesh):
    lon, obs = mesh.shape["lon"], mesh.shape["obs"]
    torus = Mesh(mesh.devices.reshape(lon // 4, 2, 2, 2, obs // 2), AXES)
    near, group = AXES[:3], AXES[3:]
    in_specs = (P(near, None), P(AXES, None), P(AXES, None), P(near, group), P())
    return jax.shard_map(
        per_device, mesh=torus, in_specs=in_specs, out_specs=P(AXES, None), check_vma=False
    )
```

```python
import functools

import jax
import jax.numpy as jnp
from jax import lax
from jax.experimental import pallas as pl
from jax.experimental.pallas import tpu as pltpu
from jax.sharding import Mesh
from jax.sharding import PartitionSpec as P

MESH = pl.DeviceIdType.MESH
BF16, F32 = jnp.bfloat16, jnp.float32
SLOTS = 7
CUTS = 4
RING_FIRST, ACROSS_FIRST = (0, 1, 3), (2,)
TURNS = ((1, 3), (2, 0), (2, 1), (0, 2), (2, 3))
LEAD = 3
TILE = 256
PARTS = 4
OUTER = (0, 1, 2, 3, -3, -2, -1)
INNER = (0, -1, 2, 1, 3, -2, -3)


def kernel(
    perturb, observed, solved, taper_index, table, out,
    x_full, x_half, obs, sol, index, rho, weighted, part, passed, joined, came, half_out, half_in, half_own, result,
    cross_in, cross_sum, ring_in,
    load_sem, obs_load_sem, sol_load_sem, index_sem, out_sem,
    obs_send, obs_recv, sol_send, sol_recv, y_send, y_recv, x_send, x_recv,
    cross_send, cross_recv, ring_send, ring_recv,
):
    z, xl, core, xh, y = (lax.axis_index(a) for a in ("z", "xl", "core", "xh", "y"))
    depth, ring = lax.axis_size("z"), lax.axis_size("y")
    rows, members = perturb.shape
    width = observed.shape[0]
    cut = width // CUTS
    span = members // PARTS
    share = rows // (2 * ring)
    way = 1 - 2 * xl
    side = 2 * core - 1
    inner = xl + core - 2 * xl * core

    mate = {"core": 1 - core}
    across = {"xl": 1 - xl}
    slant = {"z": lax.rem(z + side + depth, depth), "core": 1 - core}
    ahead = {"z": lax.rem(z + way + depth, depth)}
    behind = {"z": lax.rem(z - way + depth, depth)}
    y_up, y_down = lax.rem(y + 1, ring), lax.rem(y + ring - 1, ring)
    far = lax.rem(y + 2, ring)
    y_next = (y_up, y_down)
    opposite = {"xh": 1 - xh}

    step = rows // 4
    loads = [
        pltpu.make_async_copy(perturb.at[pl.ds(i * step, step)], x_full.at[pl.ds(i * step, step)], load_sem.at[i])
        for i in range(4)
    ]
    own_obs = pltpu.make_async_copy(observed, obs.at[pl.ds(0, width)], obs_load_sem)
    own_sol = [
        pltpu.make_async_copy(solved.at[:, pl.ds(c * span, span)], sol.at[c, pl.ds(0, width)], sol_load_sem.at[c])
        for c in range(PARTS)
    ]
    index_loads = []
    for slot in range(SLOTS):
        offset = way * (OUTER[slot] + inner * (INNER[slot] - OUTER[slot]))
        start = pl.multiple_of((offset + SLOTS // 2) * width, width)
        index_loads.append(
            pltpu.make_async_copy(taper_index.at[:, pl.ds(start, width)], index.at[slot], index_sem.at[slot])
        )

    barrier = pltpu.get_barrier_semaphore()
    peers = (mate, across, slant, ahead, behind, {"y": y_up}, {"y": y_down}, {"y": far}, opposite)
    for peer in peers:
        pl.semaphore_signal(barrier, inc=1, device_id=peer, device_id_type=MESH)
    own_obs.start()
    for slot in (0, 1):
        index_loads[slot].start()
    for i in range(4):
        loads[i].start()
    for c in range(PARTS):
        own_sol[c].start()
    for slot in (4, 2, 3, 5, 6):
        index_loads[slot].start()
    pl.semaphore_wait(barrier, len(peers))

    def remote(src, dst, send, recv, peer):
        return pltpu.make_async_remote_copy(
            src_ref=src, dst_ref=dst, send_sem=send, recv_sem=recv, device_id=peer, device_id_type=MESH
        )

    routes = {1: (0, mate), 2: (0, across), 4: (0, slant), 5: (2, ahead), 3: (2, mate), 6: (5, mate)}

    def obs_copy(slot, i):
        source, peer = routes[slot]
        src = observed.at[pl.ds(i * cut, cut)] if source == 0 else obs.at[pl.ds(source * width + i * cut, cut)]
        return remote(src, obs.at[pl.ds(slot * width + i * cut, cut)], obs_send.at[slot, i], obs_recv.at[slot, i], peer)

    def sol_copy(slot, c):
        source, peer = routes[slot]
        src = sol.at[c, pl.ds(source * width, width)]
        return remote(src, sol.at[c, pl.ds(slot * width, width)], sol_send.at[slot, c], sol_recv.at[slot, c], peer)

    obs_copies = {(slot, i): obs_copy(slot, i) for slot in routes for i in range(CUTS)}
    sol_copies = {(slot, c): sol_copy(slot, c) for slot in routes for c in range(PARTS)}

    for i in range(CUTS):
        for slot in (2, 4, 1):
            obs_copies[slot, i].start()

    levels = [table[i] * (1.0 / (members - 1)) for i in range(table.shape[0])]

    def find_rho(slot):
        index_loads[slot].wait()

        def body(i, carry):
            run = pl.ds(pl.multiple_of(i * 64, 64), 64)
            at = index[slot, run, :]
            values, bit = levels, 1
            while len(values) > 1:
                odd = (at & bit) != 0
                values = [jnp.where(odd, values[k + 1], values[k]) for k in range(0, len(values), 2)]
                bit *= 2
            rho[run, slot * width : (slot + 1) * width] = values[0]
            return carry

        lax.fori_loop(0, rows // 64, body, 0)

    def weigh(first, count):
        columns = slice(first * width, (first + count) * width)

        def body(i, carry):
            run = pl.ds(pl.multiple_of(i * TILE, TILE), TILE)
            cov = lax.dot_general(
                x_half[run, :], obs[columns, :], (((1,), (1,)), ((), ())), preferred_element_type=F32
            )
            weighted[run, columns] = (rho[run, columns] * cov).astype(BF16)
            return carry

        lax.fori_loop(0, rows // TILE, body, 0)

    def obs_came(slot):
        for i in range(CUTS):
            obs_copies[slot, i].wait_recv()

    def pass_obs(slot_from, i):
        obs_copies[slot_from, i].wait_recv()
        for slot, (source, _) in routes.items():
            if source == slot_from:
                obs_copies[slot, i].start()

    def send_sol(c):
        sol_copies[4, c].start()
        sol_copies[1, c].start()

    def pass_sol(slot_from, c):
        sol_copies[slot_from, c].wait_recv()
        for slot, (source, _) in routes.items():
            if source == slot_from:
                sol_copies[slot, c].start()

    def sol_step(c):
        send_sol(c)
        pass_sol(2, c)

    find_rho(0)
    find_rho(1)
    for i in range(4):
        loads[i].wait()

        def convert(j, carry):
            run = pl.ds(pl.multiple_of(i * step + j * 16, 16), 16)
            x_half[run, :] = x_full[run, :].astype(BF16)
            return carry

        lax.fori_loop(0, step // 16, convert, 0)
    for c in range(PARTS):
        own_sol[c].wait()
        sol_copies[2, c].start()
    own_obs.wait()
    pass_obs(2, 0)
    obs_came(1)
    weigh(0, 2)
    pass_obs(2, 1)
    find_rho(4)
    obs_came(4)
    weigh(4, 1)
    pass_obs(2, 2)
    find_rho(2)
    pass_obs(2, 3)
    find_rho(3)
    obs_came(3)
    weigh(2, 2)
    sol_step(0)
    pass_obs(5, 0)
    find_rho(5)
    pass_obs(5, 1)
    find_rho(6)
    pass_obs(5, 2)
    sol_step(1)
    pass_obs(5, 3)
    obs_came(6)
    weigh(5, 2)
    for c in range(2, LEAD):
        sol_step(c)

    def rows_of(half, where):
        return pl.ds(pl.multiple_of((half * ring + where) * share, share), share)

    def y_copy(c, way_y, kind):
        peer = {"y": y_next[way_y]}
        if kind == 0:
            src, dst = part.at[c, rows_of(way_y, far)], passed.at[c, way_y]
        elif kind == 1:
            src, dst = part.at[c, rows_of(1 - way_y, y_next[way_y])], came.at[c, way_y, 1 - way_y]
        else:
            src, dst = joined.at[c, way_y], came.at[c, way_y, way_y]
        return remote(src, dst, y_send.at[c, way_y, kind], y_recv.at[c, way_y, kind], peer)

    y_copies = {(c, w, k): y_copy(c, w, k) for c in RING_FIRST for w in range(2) for k in range(3)}
    x_copies = {
        c: remote(half_out.at[c], half_in.at[c], x_send.at[c], x_recv.at[c], opposite) for c in RING_FIRST
    }
    writes = [
        pltpu.make_async_copy(result.at[c], out.at[:, pl.ds(c * span, span)], out_sem.at[c]) for c in range(PARTS)
    ]

    def increments(c):
        def body(i, carry):
            run = pl.ds(pl.multiple_of(i * 256, 256), 256)
            total = jnp.dot(weighted[run, :], sol[c], preferred_element_type=F32)
            part[c, run, :] = total.astype(BF16)
            return carry

        lax.fori_loop(0, rows // 256, body, 0)

    def join(c):
        for w in range(2):
            y_copies[c, w, 0].wait_recv()
            joined[c, w] = (part[c, rows_of(w, y_next[w]), :].astype(F32) + passed[c, w].astype(F32)).astype(BF16)
            y_copies[c, w, 2].start()

    def gather(c):
        for w in range(2):
            for k in (1, 2):
                y_copies[c, w, k].wait_recv()

        def sum_of(half):
            mine = part[c, rows_of(half, y), :].astype(F32)
            return mine + came[c, 0, half].astype(F32) + came[c, 1, half].astype(F32)

        half_out[c] = sum_of(1 - xh).astype(BF16)
        x_copies[c].start()
        half_own[c] = sum_of(xh) + x_full[rows_of(xh, y), c * span : (c + 1) * span]

    def finish(c):
        x_copies[c].wait_recv()
        result[c] = half_own[c] + half_in[c].astype(F32)
        writes[c].start()

    places = {k: lax.rem(y + k, ring) for k in (2, 1, 3, 0)}
    cross_copies = {
        (c, k): remote(
            part.at[c, rows_of(1 - xh, places[k])], cross_in.at[c, k], cross_send.at[c, k], cross_recv.at[c, k], opposite
        )
        for c in ACROSS_FIRST
        for k in places
    }
    ring_copies = {
        (c, k): remote(cross_sum.at[c, k], ring_in.at[c, k], ring_send.at[c, k], ring_recv.at[c, k], {"y": places[k]})
        for c in ACROSS_FIRST
        for k in places
        if k
    }

    def pass_cross(c):
        for k in places:
            cross_copies[c, k].wait_recv()
            total = part[c, rows_of(xh, places[k]), :].astype(F32) + cross_in[c, k].astype(F32)
            if k:
                cross_sum[c, k] = total.astype(BF16)
                ring_copies[c, k].start()
            else:
                half_own[c] = total + x_full[rows_of(xh, y), c * span : (c + 1) * span]

    def finish_cross(c):
        total = half_own[c]
        for k in (1, 3, 2):
            ring_copies[c, k].wait_recv()
            total = total + ring_in[c, k].astype(F32)
        result[c] = total
        writes[c].start()

    for c in range(PARTS):
        pass_sol(5, c)
        for slot in (1, 3, 4, 6):
            sol_copies[slot, c].wait_recv()
        increments(c)
        if c in ACROSS_FIRST:
            for k in places:
                cross_copies[c, k].start()
        else:
            for k in range(2):
                for w in range(2):
                    y_copies[c, w, k].start()
        if c + LEAD < PARTS:
            sol_step(c + LEAD)
        if c - 1 in RING_FIRST:
            join(c - 1)
    for turn, c in TURNS:
        (pass_cross, join, gather)[turn](c)
    for c in range(PARTS):
        if c in ACROSS_FIRST:
            finish_cross(c)
        else:
            finish(c)
    for copy in (*obs_copies.values(), *sol_copies.values(), *y_copies.values(), *x_copies.values(),
                 *cross_copies.values(), *ring_copies.values()):
        copy.wait_send()
    for copy in writes:
        copy.wait()


def per_device(perturb, observed, solved, taper_index, taper_table):
    rows, members = perturb.shape
    width = observed.shape[0]
    ring = lax.axis_size("y")
    share, span = rows // (2 * ring), members // PARTS
    anywhere = pl.BlockSpec(memory_space=pl.ANY)
    dma = pltpu.SemaphoreType.DMA
    return pl.pallas_call(
        kernel,
        out_shape=jax.ShapeDtypeStruct((share, members), F32),
        in_specs=[anywhere] * 4 + [pl.BlockSpec(memory_space=pltpu.SMEM)],
        out_specs=anywhere,
        scratch_shapes=[
            pltpu.VMEM((rows, members), F32),
            pltpu.VMEM((rows, members), BF16),
            pltpu.VMEM((SLOTS * width, members), BF16),
            pltpu.VMEM((PARTS, SLOTS * width, span), BF16),
            pltpu.VMEM((SLOTS, rows, width), jnp.int32),
            pltpu.VMEM((rows, SLOTS * width), F32),
            pltpu.VMEM((rows, SLOTS * width), BF16),
            pltpu.VMEM((PARTS, rows, span), BF16),
            pltpu.VMEM((PARTS, 2, share, span), BF16),
            pltpu.VMEM((PARTS, 2, share, span), BF16),
            pltpu.VMEM((PARTS, 2, 2, share, span), BF16),
            pltpu.VMEM((PARTS, share, span), BF16),
            pltpu.VMEM((PARTS, share, span), BF16),
            pltpu.VMEM((PARTS, share, span), F32),
            pltpu.VMEM((PARTS, share, span), F32),
            pltpu.VMEM((PARTS, ring, share, span), BF16),
            pltpu.VMEM((PARTS, ring, share, span), BF16),
            pltpu.VMEM((PARTS, ring, share, span), BF16),
            dma((4,)),
            dma,
            dma((PARTS,)),
            dma((SLOTS,)),
            dma((PARTS,)),
            dma((SLOTS, CUTS)),
            dma((SLOTS, CUTS)),
            dma((SLOTS, PARTS)),
            dma((SLOTS, PARTS)),
            dma((PARTS, 2, 3)),
            dma((PARTS, 2, 3)),
            dma((PARTS,)),
            dma((PARTS,)),
            dma((PARTS, ring)),
            dma((PARTS, ring)),
            dma((PARTS, ring)),
            dma((PARTS, ring)),
        ],
        compiler_params=pltpu.CompilerParams(
            collective_id=0, has_side_effects=True, vmem_limit_bytes=50_000_000
        ),
        name="tile_update",
    )(*(pltpu.with_memory_space_constraint(a, pltpu.HBM) for a in (perturb, observed, solved, taper_index, taper_table)))


AXES = ("z", "xl", "core", "xh", "y")


def solution(mesh):
    lon, obs = mesh.shape["lon"], mesh.shape["obs"]
    torus = Mesh(mesh.devices.reshape(lon // 4, 2, 2, 2, obs // 2), AXES)
    near, group = AXES[:3], AXES[3:]
    in_specs = (P(near, None), P(AXES, None), P(AXES, None), P(near, group), P())
    return jax.shard_map(
        per_device, mesh=torus, in_specs=in_specs, out_specs=P(AXES, None), check_vma=False
    )
```

```python
import functools

import jax
import jax.numpy as jnp
from jax import lax
from jax.experimental import pallas as pl
from jax.experimental.pallas import tpu as pltpu
from jax.sharding import Mesh
from jax.sharding import PartitionSpec as P

MESH = pl.DeviceIdType.MESH
BF16, F32 = jnp.bfloat16, jnp.float32
SLOTS = 7
CUTS = 4
RING_FIRST, ACROSS_FIRST = (0, 1, 3), (2,)
TURNS = ((1, 3), (2, 0), (0, 2), (2, 1), (2, 3))
LEAD = 2
TILE = 256
PARTS = 4
OUTER = (0, 1, 2, 3, -3, -2, -1)
INNER = (0, -1, 2, 1, 3, -2, -3)


def kernel(
    perturb, observed, solved, taper_index, table, out,
    x_full, x_half, obs, sol, index, rho, weighted, part, passed, joined, came, half_out, half_in, half_own, result,
    cross_in, cross_sum, ring_in,
    load_sem, obs_load_sem, sol_load_sem, index_sem, out_sem,
    obs_send, obs_recv, sol_send, sol_recv, y_send, y_recv, x_send, x_recv,
    cross_send, cross_recv, ring_send, ring_recv,
):
    z, xl, core, xh, y = (lax.axis_index(a) for a in ("z", "xl", "core", "xh", "y"))
    depth, ring = lax.axis_size("z"), lax.axis_size("y")
    rows, members = perturb.shape
    width = observed.shape[0]
    cut = width // CUTS
    span = members // PARTS
    share = rows // (2 * ring)
    way = 1 - 2 * xl
    side = 2 * core - 1
    inner = xl + core - 2 * xl * core

    mate = {"core": 1 - core}
    across = {"xl": 1 - xl}
    slant = {"z": lax.rem(z + side + depth, depth), "core": 1 - core}
    ahead = {"z": lax.rem(z + way + depth, depth)}
    behind = {"z": lax.rem(z - way + depth, depth)}
    y_up, y_down = lax.rem(y + 1, ring), lax.rem(y + ring - 1, ring)
    far = lax.rem(y + 2, ring)
    y_next = (y_up, y_down)
    opposite = {"xh": 1 - xh}

    step = rows // 4
    loads = [
        pltpu.make_async_copy(perturb.at[pl.ds(i * step, step)], x_full.at[pl.ds(i * step, step)], load_sem.at[i])
        for i in range(4)
    ]
    own_obs = pltpu.make_async_copy(observed, obs.at[pl.ds(0, width)], obs_load_sem)
    own_sol = [
        pltpu.make_async_copy(solved.at[:, pl.ds(c * span, span)], sol.at[c, pl.ds(0, width)], sol_load_sem.at[c])
        for c in range(PARTS)
    ]
    index_loads = []
    for slot in range(SLOTS):
        offset = way * (OUTER[slot] + inner * (INNER[slot] - OUTER[slot]))
        start = pl.multiple_of((offset + SLOTS // 2) * width, width)
        index_loads.append(
            pltpu.make_async_copy(taper_index.at[:, pl.ds(start, width)], index.at[slot], index_sem.at[slot])
        )

    barrier = pltpu.get_barrier_semaphore()
    peers = (mate, across, slant, ahead, behind, {"y": y_up}, {"y": y_down}, {"y": far}, opposite)
    for peer in peers:
        pl.semaphore_signal(barrier, inc=1, device_id=peer, device_id_type=MESH)
    own_obs.start()
    for slot in (0, 1):
        index_loads[slot].start()
    for i in range(4):
        loads[i].start()
    for c in range(PARTS):
        own_sol[c].start()
    for slot in (4, 2, 3, 5, 6):
        index_loads[slot].start()
    pl.semaphore_wait(barrier, len(peers))

    def remote(src, dst, send, recv, peer):
        return pltpu.make_async_remote_copy(
            src_ref=src, dst_ref=dst, send_sem=send, recv_sem=recv, device_id=peer, device_id_type=MESH
        )

    routes = {1: (0, mate), 2: (0, across), 4: (0, slant), 5: (2, ahead), 3: (2, mate), 6: (5, mate)}

    def obs_copy(slot, i):
        source, peer = routes[slot]
        src = observed.at[pl.ds(i * cut, cut)] if source == 0 else obs.at[pl.ds(source * width + i * cut, cut)]
        return remote(src, obs.at[pl.ds(slot * width + i * cut, cut)], obs_send.at[slot, i], obs_recv.at[slot, i], peer)

    def sol_copy(slot, c):
        source, peer = routes[slot]
        src = sol.at[c, pl.ds(source * width, width)]
        return remote(src, sol.at[c, pl.ds(slot * width, width)], sol_send.at[slot, c], sol_recv.at[slot, c], peer)

    obs_copies = {(slot, i): obs_copy(slot, i) for slot in routes for i in range(CUTS)}
    sol_copies = {(slot, c): sol_copy(slot, c) for slot in routes for c in range(PARTS)}

    for i in range(CUTS):
        for slot in (2, 4, 1):
            obs_copies[slot, i].start()

    levels = [table[i] * (1.0 / (members - 1)) for i in range(table.shape[0])]

    def find_rho(slot):
        index_loads[slot].wait()

        def body(i, carry):
            run = pl.ds(pl.multiple_of(i * 64, 64), 64)
            at = index[slot, run, :]
            values, bit = levels, 1
            while len(values) > 1:
                odd = (at & bit) != 0
                values = [jnp.where(odd, values[k + 1], values[k]) for k in range(0, len(values), 2)]
                bit *= 2
            rho[run, slot * width : (slot + 1) * width] = values[0]
            return carry

        lax.fori_loop(0, rows // 64, body, 0)

    def weigh(first, count):
        columns = slice(first * width, (first + count) * width)

        def body(i, carry):
            run = pl.ds(pl.multiple_of(i * TILE, TILE), TILE)
            cov = lax.dot_general(
                x_half[run, :], obs[columns, :], (((1,), (1,)), ((), ())), preferred_element_type=F32
            )
            weighted[run, columns] = (rho[run, columns] * cov).astype(BF16)
            return carry

        lax.fori_loop(0, rows // TILE, body, 0)

    def obs_came(slot):
        for i in range(CUTS):
            obs_copies[slot, i].wait_recv()

    def pass_obs(slot_from, i):
        obs_copies[slot_from, i].wait_recv()
        for slot, (source, _) in routes.items():
            if source == slot_from:
                obs_copies[slot, i].start()

    def send_sol(c):
        sol_copies[4, c].start()
        sol_copies[1, c].start()

    def pass_sol(slot_from, c):
        sol_copies[slot_from, c].wait_recv()
        for slot, (source, _) in routes.items():
            if source == slot_from:
                sol_copies[slot, c].start()

    def sol_step(c):
        send_sol(c)
        pass_sol(2, c)

    find_rho(0)
    find_rho(1)
    for i in range(4):
        loads[i].wait()

        def convert(j, carry):
            run = pl.ds(pl.multiple_of(i * step + j * 16, 16), 16)
            x_half[run, :] = x_full[run, :].astype(BF16)
            return carry

        lax.fori_loop(0, step // 16, convert, 0)
    for c in range(PARTS):
        own_sol[c].wait()
        sol_copies[2, c].start()
    own_obs.wait()
    pass_obs(2, 0)
    obs_came(1)
    weigh(0, 2)
    pass_obs(2, 1)
    find_rho(4)
    obs_came(4)
    weigh(4, 1)
    pass_obs(2, 2)
    find_rho(2)
    pass_obs(2, 3)
    find_rho(3)
    obs_came(3)
    weigh(2, 2)
    sol_step(0)
    pass_obs(5, 0)
    find_rho(5)
    pass_obs(5, 1)
    find_rho(6)
    pass_obs(5, 2)
    sol_step(1)
    pass_obs(5, 3)
    obs_came(6)
    weigh(5, 2)
    for c in range(2, LEAD):
        sol_step(c)

    def rows_of(half, where):
        return pl.ds(pl.multiple_of((half * ring + where) * share, share), share)

    def y_copy(c, way_y, kind):
        peer = {"y": y_next[way_y]}
        if kind == 0:
            src, dst = part.at[c, rows_of(way_y, far)], passed.at[c, way_y]
        elif kind == 1:
            src, dst = part.at[c, rows_of(1 - way_y, y_next[way_y])], came.at[c, way_y, 1 - way_y]
        else:
            src, dst = joined.at[c, way_y], came.at[c, way_y, way_y]
        return remote(src, dst, y_send.at[c, way_y, kind], y_recv.at[c, way_y, kind], peer)

    y_copies = {(c, w, k): y_copy(c, w, k) for c in RING_FIRST for w in range(2) for k in range(3)}
    x_copies = {
        c: remote(half_out.at[c], half_in.at[c], x_send.at[c], x_recv.at[c], opposite) for c in RING_FIRST
    }
    writes = [
        pltpu.make_async_copy(result.at[c], out.at[:, pl.ds(c * span, span)], out_sem.at[c]) for c in range(PARTS)
    ]

    def increments(c):
        def body(i, carry):
            run = pl.ds(pl.multiple_of(i * 256, 256), 256)
            total = jnp.dot(weighted[run, :], sol[c], preferred_element_type=F32)
            part[c, run, :] = total.astype(BF16)
            return carry

        lax.fori_loop(0, rows // 256, body, 0)

    def join(c):
        for w in range(2):
            y_copies[c, w, 0].wait_recv()
            joined[c, w] = (part[c, rows_of(w, y_next[w]), :].astype(F32) + passed[c, w].astype(F32)).astype(BF16)
            y_copies[c, w, 2].start()

    def gather(c):
        for w in range(2):
            for k in (1, 2):
                y_copies[c, w, k].wait_recv()

        def sum_of(half):
            mine = part[c, rows_of(half, y), :].astype(F32)
            return mine + came[c, 0, half].astype(F32) + came[c, 1, half].astype(F32)

        half_out[c] = sum_of(1 - xh).astype(BF16)
        x_copies[c].start()
        half_own[c] = sum_of(xh) + x_full[rows_of(xh, y), c * span : (c + 1) * span]

    def finish(c):
        x_copies[c].wait_recv()
        result[c] = half_own[c] + half_in[c].astype(F32)
        writes[c].start()

    places = {k: lax.rem(y + k, ring) for k in (2, 1, 3, 0)}
    cross_copies = {
        (c, k): remote(
            part.at[c, rows_of(1 - xh, places[k])], cross_in.at[c, k], cross_send.at[c, k], cross_recv.at[c, k], opposite
        )
        for c in ACROSS_FIRST
        for k in places
    }
    ring_copies = {
        (c, k): remote(cross_sum.at[c, k], ring_in.at[c, k], ring_send.at[c, k], ring_recv.at[c, k], {"y": places[k]})
        for c in ACROSS_FIRST
        for k in places
        if k
    }

    def pass_cross(c):
        for k in places:
            cross_copies[c, k].wait_recv()
            total = part[c, rows_of(xh, places[k]), :].astype(F32) + cross_in[c, k].astype(F32)
            if k:
                cross_sum[c, k] = total.astype(BF16)
                ring_copies[c, k].start()
            else:
                half_own[c] = total + x_full[rows_of(xh, y), c * span : (c + 1) * span]

    def finish_cross(c):
        total = half_own[c]
        for k in (1, 3, 2):
            ring_copies[c, k].wait_recv()
            total = total + ring_in[c, k].astype(F32)
        result[c] = total
        writes[c].start()

    for c in range(PARTS):
        pass_sol(5, c)
        for slot in (1, 3, 4, 6):
            sol_copies[slot, c].wait_recv()
        increments(c)
        if c in ACROSS_FIRST:
            for k in places:
                cross_copies[c, k].start()
        else:
            for k in range(2):
                for w in range(2):
                    y_copies[c, w, k].start()
        if c + LEAD < PARTS:
            sol_step(c + LEAD)
        if c - 1 in RING_FIRST:
            join(c - 1)
    for turn, c in TURNS:
        (pass_cross, join, gather)[turn](c)
    for c in range(PARTS):
        if c in ACROSS_FIRST:
            finish_cross(c)
        else:
            finish(c)
    for copy in (*obs_copies.values(), *sol_copies.values(), *y_copies.values(), *x_copies.values(),
                 *cross_copies.values(), *ring_copies.values()):
        copy.wait_send()
    for copy in writes:
        copy.wait()


def per_device(perturb, observed, solved, taper_index, taper_table):
    rows, members = perturb.shape
    width = observed.shape[0]
    ring = lax.axis_size("y")
    share, span = rows // (2 * ring), members // PARTS
    anywhere = pl.BlockSpec(memory_space=pl.ANY)
    dma = pltpu.SemaphoreType.DMA
    return pl.pallas_call(
        kernel,
        out_shape=jax.ShapeDtypeStruct((share, members), F32),
        in_specs=[anywhere] * 4 + [pl.BlockSpec(memory_space=pltpu.SMEM)],
        out_specs=anywhere,
        scratch_shapes=[
            pltpu.VMEM((rows, members), F32),
            pltpu.VMEM((rows, members), BF16),
            pltpu.VMEM((SLOTS * width, members), BF16),
            pltpu.VMEM((PARTS, SLOTS * width, span), BF16),
            pltpu.VMEM((SLOTS, rows, width), jnp.int32),
            pltpu.VMEM((rows, SLOTS * width), F32),
            pltpu.VMEM((rows, SLOTS * width), BF16),
            pltpu.VMEM((PARTS, rows, span), BF16),
            pltpu.VMEM((PARTS, 2, share, span), BF16),
            pltpu.VMEM((PARTS, 2, share, span), BF16),
            pltpu.VMEM((PARTS, 2, 2, share, span), BF16),
            pltpu.VMEM((PARTS, share, span), BF16),
            pltpu.VMEM((PARTS, share, span), BF16),
            pltpu.VMEM((PARTS, share, span), F32),
            pltpu.VMEM((PARTS, share, span), F32),
            pltpu.VMEM((PARTS, ring, share, span), BF16),
            pltpu.VMEM((PARTS, ring, share, span), BF16),
            pltpu.VMEM((PARTS, ring, share, span), BF16),
            dma((4,)),
            dma,
            dma((PARTS,)),
            dma((SLOTS,)),
            dma((PARTS,)),
            dma((SLOTS, CUTS)),
            dma((SLOTS, CUTS)),
            dma((SLOTS, PARTS)),
            dma((SLOTS, PARTS)),
            dma((PARTS, 2, 3)),
            dma((PARTS, 2, 3)),
            dma((PARTS,)),
            dma((PARTS,)),
            dma((PARTS, ring)),
            dma((PARTS, ring)),
            dma((PARTS, ring)),
            dma((PARTS, ring)),
        ],
        compiler_params=pltpu.CompilerParams(
            collective_id=0, has_side_effects=True, vmem_limit_bytes=50_000_000
        ),
        name="tile_update",
    )(*(pltpu.with_memory_space_constraint(a, pltpu.HBM) for a in (perturb, observed, solved, taper_index, taper_table)))


AXES = ("z", "xl", "core", "xh", "y")


def solution(mesh):
    lon, obs = mesh.shape["lon"], mesh.shape["obs"]
    torus = Mesh(mesh.devices.reshape(lon // 4, 2, 2, 2, obs // 2), AXES)
    near, group = AXES[:3], AXES[3:]
    in_specs = (P(near, None), P(AXES, None), P(AXES, None), P(near, group), P())
    return jax.shard_map(
        per_device, mesh=torus, in_specs=in_specs, out_specs=P(AXES, None), check_vma=False
    )
```
